32 devices in a mesh: fsdp: 8 (over y, x, core), tp: 4 (over z).
Axes of the slice: x: 2, y: 2, z: 4, core: 2. Of those that a mesh axis runs over, the one named last changes fastest.
Arguments:
- pool: bfloat16 [1024, 16384], P(None, 'fsdp'), may hold values from -6 to 6
- ids: int32 [2, 384], replicated, may hold values from 0 to 1023, as said below
- gate_q: bfloat16 [26624, 16384], P(('fsdp', 'tp')), may hold values from -240 to 240, as said below
- up_q: bfloat16 [26624, 16384], P(('fsdp', 'tp')), may hold values from -240 to 240, as said below
- gate_scale: float32 [208, 128], replicated, may hold values from 3e-05 to 0.0003
- up_scale: float32 [208, 128], replicated, may hold values from 3e-05 to 0.0003
- down_weight: bfloat16 [26624, 16384], P('tp', 'fsdp'), may hold values from -0.0390625 to 0.0390625
Outputs:
- mixed: bfloat16 [2, 384, 16384], P(None, 'tp', 'fsdp')
The draws below stay inside these ranges and needn't reach their ends.
Inputs may be any that keep to these rules, and one draw needn't show every extreme that they name: All 768 ids are different: no request is decoded twice. `gate_q`: every entry is a value of the 8-bit float form e4m3: a sign times (1 + k / 8) times 2 to the power e, with whole k of 0 to 7 and whole e of 0 to 7. `up_q`: every entry is a value of the 8-bit float form e4m3: a sign times (1 + k / 8) times 2 to the power e, with whole k of 0 to 7 and whole e of 0 to 7.
All inputs are finite; a program needn't handle non-finite values.
Results may differ from the reference program's by a relative error of at most 0.0065.
Values may be sent and summed in bfloat16 or wider, within the bound.
No kernel may reach another device: no remote copies, remote signals or barrier semaphores. Data moves between devices by JAX's collectives and lax.ppermute only.
A program may use at most 448 MiB of HBM per device.

```python
import math
import jax
import jax.numpy as jnp

D = 16384
FF = 26624
BLOCK = 128
STEPS = 2
ROWS = 384
POOL = 1024


def e4m3_values(key):
    key_sign, key_expo, key_mant = jax.random.split(key, 3)
    signs = 2 * jax.random.randint(key_sign, (FF, D), 0, 2, dtype=jnp.int32) - 1
    exponent = jax.random.randint(key_expo, (FF, D), 0, 8, dtype=jnp.int32)
    mantissa = jax.random.randint(key_mant, (FF, D), 0, 8, dtype=jnp.int32)
    powers = jnp.array([1.0, 2.0, 4.0, 8.0, 16.0, 32.0, 64.0, 128.0], dtype=jnp.float32)
    magnitude = (1.0 + mantissa.astype(jnp.float32) / 8.0) * jnp.take(powers, exponent)
    return (signs.astype(jnp.float32) * magnitude).astype(jnp.bfloat16)


def draw_gate_q(key, part):
    return e4m3_values(jax.random.fold_in(key, 11))


def draw_up_q(key, part):
    return e4m3_values(jax.random.fold_in(key, 23))


def draw_ids(key, part):
    key_order = jax.random.fold_in(key, 37)
    key_shuffle = jax.random.fold_in(key, 41)
    scores = jax.random.permutation(key_order, POOL).astype(jnp.int32)
    scores = scores.at[0].set(-2).at[POOL - 1].set(-1)
    ranked = jnp.argsort(scores, stable=True).astype(jnp.int32)
    chosen = ranked[:STEPS * ROWS]
    placing = jax.random.permutation(key_shuffle, STEPS * ROWS).astype(jnp.int32)
    return jnp.take(chosen, placing).reshape(STEPS, ROWS).astype(jnp.int32)


def shard_levels(stream_key, extent, pieces, low, top_value):
    gain = 1.0
    for dim, parts in pieces:
        steps = jax.random.uniform(jax.random.fold_in(jax.random.fold_in(stream_key, 6), dim), (parts,), jnp.float32, low / len(pieces), top_value / len(pieces))
        gain = gain * jnp.repeat(jnp.exp(steps), extent[dim] // parts).reshape((-1,) + (1,) * (len(extent) - 1 - dim))
    return gain


def normal_values(key, dims, spread, limit, cuts=(), held_as=jnp.bfloat16):
    result = spread * jax.random.normal(key, dims, jnp.float32)
    if cuts:
        result = result * shard_levels(key, dims, cuts, -0.22, 0.18)
    return jnp.clip(result, -limit, limit).astype(held_as)


def setup_inputs(seed: int = 0) -> dict:
    keys = jax.random.split(jax.random.key(seed), 8)
    return {
        "pool": normal_values(keys[0], (POOL, D), 1.0, 6.0, ((1, 8),)),
        "ids": draw_ids(jax.random.fold_in(keys[7], 71), 0),
        "gate_q": draw_gate_q(jax.random.fold_in(keys[7], 71), 0),
        "up_q": draw_up_q(jax.random.fold_in(keys[7], 71), 0),
        "gate_scale": jnp.clip(jnp.exp(jax.random.uniform(keys[4], (FF // BLOCK, D // BLOCK), jnp.float32, math.log(2.9999999242136255e-05), math.log(0.0003))), 2.9999999242136255e-05, 0.0003),
        "up_scale": jnp.clip(jnp.exp(jax.random.uniform(keys[5], (FF // BLOCK, D // BLOCK), jnp.float32, math.log(2.9999999242136255e-05), math.log(0.0003))), 2.9999999242136255e-05, 0.0003),
        "down_weight": normal_values(keys[6], (FF, D), FF ** -0.5, 0.0390625, ((0, 4), (1, 8))),
    }


def dequantize(quant, scale):
    blocks = quant.astype(jnp.float32).reshape(FF // BLOCK, BLOCK, D // BLOCK, BLOCK)
    return (blocks * scale[:, None, :, None]).astype(jnp.bfloat16).reshape(FF, D)


def reference(pool, ids, gate_q, up_q, gate_scale, up_scale, down_weight):
    gate_w = dequantize(gate_q, gate_scale)
    up_w = dequantize(up_q, up_scale)
    results = []
    for step in range(STEPS):
        tokens = jnp.take(pool, ids[step].astype(jnp.int32), axis=0)
        gate = jnp.dot(tokens, gate_w.T, preferred_element_type=jnp.float32)
        up = jnp.dot(tokens, up_w.T, preferred_element_type=jnp.float32)
        hidden = (jax.nn.silu(gate) * up).astype(jnp.bfloat16)
        results.append(jnp.dot(hidden, down_weight, preferred_element_type=jnp.float32).astype(jnp.bfloat16))
    return jnp.stack(results)
```

```python
import functools
import math

import jax
import jax.numpy as jnp
from jax import lax
from jax.experimental import pallas as pl
from jax.experimental.pallas import tpu as pltpu
from jax.experimental.layout import Layout, with_layout_constraint
from jax.sharding import PartitionSpec as P

BLOCK = 128
HALVES = 2
LANES = 128
VMEM_BYTES = 32 << 20
CHUNKS = (2, 1)


def rows_first(x):
    return with_layout_constraint(x, Layout(major_to_minor=tuple(range(x.ndim))))


def swap(block, mask):
    n = lax.axis_size("fsdp")
    moved = lax.ppermute(rows_first(block), "fsdp", [(i, i ^ mask) for i in range(n)])
    return rows_first(moved)


def shift(block, by):
    n = lax.axis_size("tp")
    moved = lax.ppermute(rows_first(block), "tp", [(i, (i + by) % n) for i in range(n)])
    return rows_first(moved)


def after(values, *others):
    return lax.optimization_barrier((values, others))[0]


def flips():
    masks, bit = [], 2
    while bit < lax.axis_size("fsdp"):
        masks.append(bit)
        bit *= 2
    return masks


def last_flips(mask):
    flip_list = flips()
    routes = []
    for i in range(HALVES):
        turn = i % len(flip_list)
        order = flip_list[turn:] + flip_list[:turn]
        routes.append([d for d in order if d & mask][-1])
    return routes


def levels():
    masks = range(2, lax.axis_size("fsdp"), 2)
    return [[r for r in masks if r.bit_count() == n] for n in range(1, len(flips()) + 1)]


def spread(got, level, axis):
    def part(pieces, i):
        if len(pieces) > 1:
            return pieces[i]
        size = pieces[0].shape[axis] // HALVES
        return lax.slice_in_dim(pieces[0], i * size, (i + 1) * size, axis=axis)

    for r in level:
        if r.bit_count() == 1:
            got[r] = [swap(got[0][0], r)]
        else:
            got[r] = [swap(part(got[r ^ d], i), d) for i, d in enumerate(last_flips(r))]


def other_core(pieces):
    return [swap(p, 1) for p in pieces]


def when_step(step, n, action):
    for i in range(n):

        @pl.when(step == i)
        def _(i=i):
            action(i)


def gate_up_kernel(parts, first, last, g, idx, *refs):
    n = len(parts)
    n_arrays = 1 + max(a for a, _ in parts)
    xs, refs = refs[:n_arrays], refs[n_arrays:]
    gq, uq, gs, us, refs = *refs[:4], refs[4:]
    if not first:
        acc, refs = refs[0], refs[1:]
    if last:
        out, w, xb, sem = refs
    elif first:
        acc, w, xb, sem = refs
    else:
        _, w, xb, sem = refs
    k = pl.program_id(0)
    tk = xb.shape[2]
    rows = gq.shape[0]

    def copy(i):
        a, part = parts[i]
        return pltpu.make_async_copy(
            xs[a].at[:, pl.ds(part * tk, tk)], xb.at[i % 2], sem.at[i % 2]
        )

    @pl.when(k == 0)
    def _():
        copy(0).start()
        if first:
            acc[...] = jnp.zeros_like(acc)

    when_step(k + 1, n, lambda i: copy(i).start())
    slot = lax.rem(k, 2)
    for i, (q, s) in enumerate(((gq, gs), (uq, us))):
        for j in range(rows // g):
            w[i * rows + j * g : i * rows + (j + 1) * g, :] = (
                q[j * g : (j + 1) * g, :].astype(jnp.float32) * s[j : j + 1, :]
            ).astype(jnp.bfloat16)
    pltpu.make_async_copy(
        xs[0].at[:, pl.ds(0, tk)], xb.at[slot], sem.at[slot]
    ).wait()
    acc[...] += lax.dot_general(
        w[...], xb[slot], (((1,), (1,)), ((), ())), preferred_element_type=jnp.float32
    )
    if last:

        @pl.when(k == n - 1)
        def _():
            gate = acc[:rows, :]
            hidden = gate / (1.0 + jnp.exp(-gate)) * acc[rows:, :]
            out[:, :rows] = hidden.T.astype(out.dtype)
            if out.shape[1] > rows:
                out[:, rows:] = jnp.zeros((out.shape[0], out.shape[1] - rows), out.dtype)


def gate_up(tk, arrays, parts, at, columns, weights, acc, last):
    m = arrays[0].shape[0]
    gate_q, _, gate_s, _ = weights
    rows = gate_q.shape[0]
    n = len(parts)
    groups = gate_s.shape[0]
    quant = pl.BlockSpec((rows, tk), lambda k, idx: (0, idx[k + at]))
    scale = pl.BlockSpec((groups, tk), lambda k, idx: (0, idx[k + at]))
    in_specs = [pl.BlockSpec(memory_space=pl.ANY)] * len(arrays)
    in_specs += [quant, quant, scale, scale]
    operands = [*arrays, *weights]
    aliases = {}
    if acc is not None:
        in_specs.append(pl.BlockSpec(memory_space=pltpu.VMEM))
        operands.append(acc)
        if not last:
            aliases = {len(operands): 0}
    scratch = [
        pltpu.VMEM((2 * rows, tk), jnp.bfloat16),
        pltpu.VMEM((2, m, tk), jnp.bfloat16),
        pltpu.SemaphoreType.DMA((2,)),
    ]
    if last:
        padded = pl.cdiv(rows, LANES) * LANES
        out_specs = pl.BlockSpec((m, padded), lambda k, idx: (0, 0))
        out_shape = jax.ShapeDtypeStruct((m, padded), jnp.bfloat16)
    else:
        out_specs = pl.BlockSpec(memory_space=pltpu.VMEM)
        out_shape = jax.ShapeDtypeStruct((2 * rows, m), jnp.float32)
    return pl.pallas_call(
        functools.partial(gate_up_kernel, parts, acc is None, last, rows // groups),
        grid_spec=pltpu.PrefetchScalarGridSpec(
            num_scalar_prefetch=1,
            grid=(n,),
            in_specs=in_specs,
            out_specs=out_specs,
            scratch_shapes=scratch,
        ),
        out_shape=out_shape,
        input_output_aliases=aliases,
        cost_estimate=pl.CostEstimate(
            flops=4 * m * rows * tk * n,
            bytes_accessed=4 * rows * tk * n,
            transcendentals=0,
        ),
        compiler_params=pltpu.CompilerParams(
            dimension_semantics=("arbitrary",), vmem_limit_bytes=VMEM_BYTES
        ),
    )(columns, *operands)


def down_kernel(sources, n_tp, idx, *refs):
    n_arrays = 1 + max(a for parts in sources for a, _ in parts)
    xs, (dw, out, acc, xb, sem) = refs[:n_arrays], refs[n_arrays:]
    n = len(sources)
    members = len(sources[0])
    pm = xb.shape[1] // members
    rr = pm // n_tp
    k = pl.program_id(0)

    def start(i):
        for r, (a, row) in enumerate(sources[i]):
            pltpu.make_async_copy(
                xs[a].at[pl.ds(row, pm), :],
                xb.at[i % 2, pl.ds(r * pm, pm), :],
                sem.at[i % 2, r],
            ).start()

    @pl.when(k == 0)
    def _():
        start(0)
        acc[...] = jnp.zeros_like(acc)

    when_step(k + 1, n, start)
    slot = lax.rem(k, 2)
    for r in range(members):
        pltpu.make_async_copy(
            xs[0].at[pl.ds(0, pm), :], xb.at[slot, pl.ds(r * pm, pm), :], sem.at[slot, r]
        ).wait()
    acc[...] += jnp.dot(
        xb[slot, :, : dw.shape[0]], dw[...], preferred_element_type=jnp.float32
    )

    @pl.when(k == n - 1)
    def _():
        for to in range(n_tp):
            for r in range(members):
                a, b = r * pm + to * rr, (to * members + r) * rr
                out[b : b + rr, :] = acc[a : a + rr, :].astype(out.dtype)


def down(n_tp, rows, arrays, sources, pm, chunks, down_weight):
    padded = arrays[0].shape[1]
    m = pm * len(sources[0])
    width = down_weight.shape[1]
    n = len(sources)
    return pl.pallas_call(
        functools.partial(down_kernel, sources, n_tp),
        grid_spec=pltpu.PrefetchScalarGridSpec(
            num_scalar_prefetch=1,
            grid=(n,),
            in_specs=[pl.BlockSpec(memory_space=pl.ANY)] * len(arrays)
            + [pl.BlockSpec((rows, width), lambda k, idx: (idx[k], 0))],
            out_specs=pl.BlockSpec((m, width), lambda k, idx: (0, 0)),
            scratch_shapes=[
                pltpu.VMEM((m, width), jnp.float32),
                pltpu.VMEM((2, m, padded), jnp.bfloat16),
                pltpu.SemaphoreType.DMA((2, len(sources[0]))),
            ],
        ),
        out_shape=jax.ShapeDtypeStruct((m, width), jnp.bfloat16),
        cost_estimate=pl.CostEstimate(
            flops=2 * m * rows * width * n,
            bytes_accessed=2 * rows * width * n,
            transcendentals=0,
        ),
        compiler_params=pltpu.CompilerParams(
            dimension_semantics=("arbitrary",), vmem_limit_bytes=VMEM_BYTES
        ),
    )(chunks, *arrays, down_weight)


def on_device(pool, ids, gate_q, up_q, gate_scale, up_scale, down_weight):
    n_fsdp = lax.axis_size("fsdp")
    n_tp = lax.axis_size("tp")
    f = lax.axis_index("fsdp")
    t = lax.axis_index("tp")
    rows_here = gate_q.shape[0]
    width = pool.shape[1]
    steps, step_rows = ids.shape
    members = n_fsdp // 2
    spans = n_fsdp // n_tp // 2
    q = f // 2
    core = f % 2
    near = levels()
    masks = [0] + [r for level in near for r in level]

    g = math.gcd(rows_here, BLOCK)
    row_blocks = (
        (f * n_tp + t) * rows_here + g * jnp.arange(rows_here // g, dtype=jnp.int32)
    ) // BLOCK
    weights = (gate_q, up_q) + tuple(
        jnp.repeat(jnp.take(s, row_blocks, axis=0), BLOCK, axis=1)
        for s in (gate_scale, up_scale)
    )

    share = steps * step_rows // n_tp
    by_owner = ids.reshape(steps, n_tp, step_rows // n_tp).transpose(1, 0, 2)
    by_owner = by_owner.reshape(n_tp, share)
    requests = jnp.arange(pool.shape[0], dtype=jnp.int32)

    def pick(begin, end):
        rr = (end - begin) // members
        named = by_owner[:, begin:end].reshape(n_tp, members, rr).transpose(1, 0, 2)
        chosen = (named.reshape(-1, 1) == requests).astype(jnp.bfloat16)
        picked = jnp.dot(chosen, pool, preferred_element_type=jnp.float32)
        return picked.astype(jnp.bfloat16)

    halves = jnp.arange(HALVES, dtype=jnp.int32)

    def columns_of(masks_in_order):
        flipped = f ^ jnp.array(masks_in_order, dtype=jnp.int32)
        return (flipped[:, None] * HALVES + halves).reshape(-1)

    visits = [0, 1]
    for c in range(2):
        visits += [r ^ c for r in near[0]]
    for c in range(2):
        visits += [r ^ c for level in near[1:] for r in level]
    columns = columns_of(visits)

    def gate_up_part(wanted, acc, last):
        arrays, parts = [], []
        for r, c, pieces in wanted:
            for p in pieces:
                for j in range(HALVES // len(pieces)):
                    parts.append((len(arrays), j))
                arrays.append(p)
        r, c, _ = wanted[0]
        at = visits.index(r ^ c) * HALVES
        return gate_up(
            width // HALVES, arrays, tuple(parts), at, columns, weights, acc, last
        )

    def scatter(hidden):
        pm = hidden.shape[0] // members
        pieces = [
            lax.dynamic_slice_in_dim(hidden, (q ^ (r // 2)) * pm, pm, axis=0)
            for r in range(0, n_fsdp, 2)
        ]
        return [swap(p, 2 * i) if i else p for i, p in enumerate(pieces)]

    def to_planes(pieces):
        pieces = jnp.stack(pieces)
        arrived = []
        for dz in range(n_tp):
            to = (t + dz) % n_tp
            for v in range(spans):
                piece = lax.dynamic_index_in_dim(
                    pieces, q ^ (to * spans + v), 0, keepdims=False
                )
                arrived.append(shift(piece, dz) if dz else piece)
        return arrived

    def down_part(by_core):
        n_here = n_tp * spans
        pm = by_core[0][0][0].shape[0] // n_here
        arrays, where, sources, chunks = [], {}, [], []
        for c, got in enumerate(by_core):
            for r in masks:
                where[c, r] = (len(arrays), len(got[r]))
                arrays.extend(got[r])
        for c in range(2):
            for i in range(n_here):
                parts = []
                for r in masks:
                    a, held = where[c, r]
                    each = n_here // held
                    parts.append((a + i // each, (i % each) * pm))
                sources.append(tuple(parts))
                dz, v = divmod(i, spans)
                chunks.append((2 * v + (core ^ c)) * n_tp + (t - dz) % n_tp)
        chunks = jnp.stack(chunks).astype(jnp.int32)
        return down(n_tp, rows_here, arrays, tuple(sources), pm, chunks, down_weight)

    def exchange(partial):
        rows = partial.shape[0] // n_tp
        shares = [
            lax.dynamic_slice_in_dim(partial, (t + dz) % n_tp * rows, rows, axis=0)
            for dz in range(n_tp)
        ]
        return [shift(s, dz) if dz else s for dz, s in enumerate(shares)]

    def total(shares):
        summed = functools.reduce(jnp.add, [s.astype(jnp.float32) for s in shares])
        rr = summed.shape[0] // members
        summed = summed.astype(jnp.bfloat16).reshape(members, rr, width)
        place = {r: i for i, r in enumerate(masks)}
        back = jnp.array([place[2 * i] for i in range(members)], dtype=jnp.int32)
        ordered = [
            lax.dynamic_index_in_dim(summed, back[q ^ i], 0, keepdims=False)
            for i in range(members)
        ]
        return jnp.concatenate(ordered)

    n = len(CHUNKS)
    ends = [share * sum(CHUNKS[: i + 1]) // sum(CHUNKS) for i in range(n)]
    own = [pick(b, e) for b, e in zip([0] + ends[:-1], ends)]
    tokens = [{0: [x]} for x in own]

    far = [r for level in near[1:] for r in level]

    def blocks_of(got, group):
        return [got[r] for r in group]

    def hold(got, group, *others):
        for r, held in zip(group, after(blocks_of(got, group), *others)):
            got[r] = held

    def far_blocks(got, axis):
        for level in near[1:]:
            spread(got, level, axis)

    def land(pieces):
        got = {0: [jnp.concatenate(pieces)]}
        spread(got, near[0], 0)
        return got

    def twins_of(got, group):
        return {r: other_core(got[r]) for r in group}

    def hold_all(pieces, *others):
        held = after([p for _, _, p in pieces], *others)
        return [(r, c, p) for (r, c, _), p in zip(pieces, held)]

    def wanted(got, core_flip, group):
        return [(r, core_flip, got[r]) for r in group]

    first, last = tokens

    spread(first, near[0], 1)
    here = [wanted(x, 0, [0]) + wanted(twins_of(x, [0]), 1, [0]) for x in tokens]
    acc_first = gate_up_part(here[0], None, False)
    acc_last = gate_up_part(hold_all(here[1], acc_first), None, False)

    hold(first, near[0], acc_last)
    far_blocks(first, 1)
    twins = twins_of(first, near[0])
    last[0] = after(last[0], blocks_of(first, near[0]))
    spread(last, near[0], 1)
    acc_first = gate_up_part(wanted(first, 0, near[0]), acc_first, False)
    acc_first = gate_up_part(wanted(twins, 1, near[0]), acc_first, False)
    hold(first, far, acc_first)
    pieces = wanted(first, 0, far) + wanted(twins_of(first, far), 1, far)
    hidden_first = gate_up_part(pieces, acc_first, True)
    moved_first = scatter(hidden_first)

    hold(last, near[0], hidden_first)
    far_blocks(last, 1)
    twins = twins_of(last, near[0])
    moved_first = to_planes(after(moved_first, blocks_of(last, near[0])))
    pieces = wanted(last, 0, near[0]) + wanted(twins, 1, near[0])
    acc_last = gate_up_part(hold_all(pieces, moved_first[0]), acc_last, False)
    hold(last, far, acc_last)
    twins = twins_of(last, far)
    landed_first = land(after(moved_first, acc_last))
    pieces = wanted(last, 0, far) + wanted(twins, 1, far)
    hidden_last = gate_up_part(pieces, acc_last, True)
    moved_last = scatter(hidden_last)

    hold(landed_first, near[0], hidden_last)
    far_blocks(landed_first, 0)
    twins = twins_of(landed_first, [0] + near[0])
    moved_last = to_planes(after(moved_last, blocks_of(landed_first, near[0])))
    twins.update(twins_of(landed_first, far))
    partial_first = down_part((landed_first, twins))
    shares_first = exchange(partial_first)
    landed_last = land(after(moved_last, shares_first[0]))

    hold(landed_last, near[0], partial_first)
    far_blocks(landed_last, 0)
    twins = twins_of(landed_last, masks)
    partial_last = down_part((landed_last, twins))
    shares_last = exchange(partial_last)
    shares_first, shares_last = after((shares_first, shares_last))
    mixed = [total(shares_first), total(shares_last)]
    return jnp.concatenate(mixed).reshape(steps, share // steps, width)


def solution(mesh):
    in_specs = (
        P(None, "fsdp"),
        P(),
        P(("fsdp", "tp"), None),
        P(("fsdp", "tp"), None),
        P(),
        P(),
        P("tp", "fsdp"),
    )
    out_specs = P(None, "tp", "fsdp")

    return jax.shard_map(
        on_device, mesh=mesh, in_specs=in_specs, out_specs=out_specs, check_vma=False
    )
```

```python
import functools
import math

import jax
import jax.numpy as jnp
from jax import lax
from jax.experimental import pallas as pl
from jax.experimental.pallas import tpu as pltpu
from jax.experimental.layout import Layout, with_layout_constraint
from jax.sharding import PartitionSpec as P

BLOCK = 128
HALVES = 2
LANES = 128
VMEM_BYTES = 32 << 20
CHUNKS = (2, 1)


def rows_first(x):
    return with_layout_constraint(x, Layout(major_to_minor=tuple(range(x.ndim))))


def swap(block, mask):
    n = lax.axis_size("fsdp")
    moved = lax.ppermute(rows_first(block), "fsdp", [(i, i ^ mask) for i in range(n)])
    return rows_first(moved)


def shift(block, by):
    n = lax.axis_size("tp")
    moved = lax.ppermute(rows_first(block), "tp", [(i, (i + by) % n) for i in range(n)])
    return rows_first(moved)


def after(values, *others):
    return lax.optimization_barrier((values, others))[0]


def flips():
    masks, bit = [], 2
    while bit < lax.axis_size("fsdp"):
        masks.append(bit)
        bit *= 2
    return masks


def last_flips(mask):
    flip_list = flips()
    routes = []
    for i in range(HALVES):
        turn = i % len(flip_list)
        order = flip_list[turn:] + flip_list[:turn]
        routes.append([d for d in order if d & mask][-1])
    return routes


def levels():
    masks = range(2, lax.axis_size("fsdp"), 2)
    return [[r for r in masks if r.bit_count() == n] for n in range(1, len(flips()) + 1)]


def spread(got, level, axis):
    def part(pieces, i):
        if len(pieces) > 1:
            return pieces[i]
        size = pieces[0].shape[axis] // HALVES
        return lax.slice_in_dim(pieces[0], i * size, (i + 1) * size, axis=axis)

    for r in level:
        if r.bit_count() == 1:
            got[r] = [swap(p, r) for p in got[0]]
        else:
            got[r] = [swap(part(got[r ^ d], i), d) for i, d in enumerate(last_flips(r))]


def other_core(pieces):
    return [swap(p, 1) for p in pieces]


def when_step(step, n, action):
    for i in range(n):

        @pl.when(step == i)
        def _(i=i):
            action(i)


def gate_up_kernel(parts, first, last, g, idx, *refs):
    n = len(parts)
    n_arrays = 1 + max(a for a, _ in parts)
    xs, refs = refs[:n_arrays], refs[n_arrays:]
    gq, uq, gs, us, refs = *refs[:4], refs[4:]
    if not first:
        acc, refs = refs[0], refs[1:]
    if last:
        out, w, xb, sem = refs
    elif first:
        acc, w, xb, sem = refs
    else:
        _, w, xb, sem = refs
    k = pl.program_id(0)
    tk = xb.shape[2]
    rows = gq.shape[0]

    def copy(i):
        a, part = parts[i]
        return pltpu.make_async_copy(
            xs[a].at[:, pl.ds(part * tk, tk)], xb.at[i % 2], sem.at[i % 2]
        )

    @pl.when(k == 0)
    def _():
        copy(0).start()
        if first:
            acc[...] = jnp.zeros_like(acc)

    when_step(k + 1, n, lambda i: copy(i).start())
    slot = lax.rem(k, 2)
    for i, (q, s) in enumerate(((gq, gs), (uq, us))):
        for j in range(rows // g):
            w[i * rows + j * g : i * rows + (j + 1) * g, :] = (
                q[j * g : (j + 1) * g, :].astype(jnp.float32) * s[j : j + 1, :]
            ).astype(jnp.bfloat16)
    pltpu.make_async_copy(
        xs[0].at[:, pl.ds(0, tk)], xb.at[slot], sem.at[slot]
    ).wait()
    acc[...] += lax.dot_general(
        w[...], xb[slot], (((1,), (1,)), ((), ())), preferred_element_type=jnp.float32
    )
    if last:

        @pl.when(k == n - 1)
        def _():
            gate = acc[:rows, :]
            hidden = gate / (1.0 + jnp.exp(-gate)) * acc[rows:, :]
            out[:, :rows] = hidden.T.astype(out.dtype)
            if out.shape[1] > rows:
                out[:, rows:] = jnp.zeros((out.shape[0], out.shape[1] - rows), out.dtype)


def gate_up(tk, arrays, parts, at, columns, weights, acc, last):
    m = arrays[0].shape[0]
    gate_q, _, gate_s, _ = weights
    rows = gate_q.shape[0]
    n = len(parts)
    groups = gate_s.shape[0]
    quant = pl.BlockSpec((rows, tk), lambda k, idx: (0, idx[k + at]))
    scale = pl.BlockSpec((groups, tk), lambda k, idx: (0, idx[k + at]))
    in_specs = [pl.BlockSpec(memory_space=pl.ANY)] * len(arrays)
    in_specs += [quant, quant, scale, scale]
    operands = [*arrays, *weights]
    aliases = {}
    if acc is not None:
        in_specs.append(pl.BlockSpec(memory_space=pltpu.VMEM))
        operands.append(acc)
        if not last:
            aliases = {len(operands): 0}
    scratch = [
        pltpu.VMEM((2 * rows, tk), jnp.bfloat16),
        pltpu.VMEM((2, m, tk), jnp.bfloat16),
        pltpu.SemaphoreType.DMA((2,)),
    ]
    if last:
        padded = pl.cdiv(rows, LANES) * LANES
        out_specs = pl.BlockSpec((m, padded), lambda k, idx: (0, 0))
        out_shape = jax.ShapeDtypeStruct((m, padded), jnp.bfloat16)
    else:
        out_specs = pl.BlockSpec(memory_space=pltpu.VMEM)
        out_shape = jax.ShapeDtypeStruct((2 * rows, m), jnp.float32)
    return pl.pallas_call(
        functools.partial(gate_up_kernel, parts, acc is None, last, rows // groups),
        grid_spec=pltpu.PrefetchScalarGridSpec(
            num_scalar_prefetch=1,
            grid=(n,),
            in_specs=in_specs,
            out_specs=out_specs,
            scratch_shapes=scratch,
        ),
        out_shape=out_shape,
        input_output_aliases=aliases,
        cost_estimate=pl.CostEstimate(
            flops=4 * m * rows * tk * n,
            bytes_accessed=4 * rows * tk * n,
            transcendentals=0,
        ),
        compiler_params=pltpu.CompilerParams(
            dimension_semantics=("arbitrary",), vmem_limit_bytes=VMEM_BYTES
        ),
    )(columns, *operands)


def down_kernel(sources, n_tp, idx, *refs):
    n_arrays = 1 + max(a for parts in sources for a, _ in parts)
    xs, (dw, out, acc, xb, sem) = refs[:n_arrays], refs[n_arrays:]
    n = len(sources)
    members = len(sources[0])
    pm = xb.shape[1] // members
    rr = pm // n_tp
    k = pl.program_id(0)

    def start(i):
        for r, (a, row) in enumerate(sources[i]):
            pltpu.make_async_copy(
                xs[a].at[pl.ds(row, pm), :],
                xb.at[i % 2, pl.ds(r * pm, pm), :],
                sem.at[i % 2, r],
            ).start()

    @pl.when(k == 0)
    def _():
        start(0)
        acc[...] = jnp.zeros_like(acc)

    when_step(k + 1, n, start)
    slot = lax.rem(k, 2)
    for r in range(members):
        pltpu.make_async_copy(
            xs[0].at[pl.ds(0, pm), :], xb.at[slot, pl.ds(r * pm, pm), :], sem.at[slot, r]
        ).wait()
    acc[...] += jnp.dot(
        xb[slot, :, : dw.shape[0]], dw[...], preferred_element_type=jnp.float32
    )

    @pl.when(k == n - 1)
    def _():
        for to in range(n_tp):
            for r in range(members):
                a, b = r * pm + to * rr, (to * members + r) * rr
                out[b : b + rr, :] = acc[a : a + rr, :].astype(out.dtype)


def down(n_tp, rows, arrays, sources, pm, chunks, down_weight):
    padded = arrays[0].shape[1]
    m = pm * len(sources[0])
    width = down_weight.shape[1]
    n = len(sources)
    return pl.pallas_call(
        functools.partial(down_kernel, sources, n_tp),
        grid_spec=pltpu.PrefetchScalarGridSpec(
            num_scalar_prefetch=1,
            grid=(n,),
            in_specs=[pl.BlockSpec(memory_space=pl.ANY)] * len(arrays)
            + [pl.BlockSpec((rows, width), lambda k, idx: (idx[k], 0))],
            out_specs=pl.BlockSpec((m, width), lambda k, idx: (0, 0)),
            scratch_shapes=[
                pltpu.VMEM((m, width), jnp.float32),
                pltpu.VMEM((2, m, padded), jnp.bfloat16),
                pltpu.SemaphoreType.DMA((2, len(sources[0]))),
            ],
        ),
        out_shape=jax.ShapeDtypeStruct((m, width), jnp.bfloat16),
        cost_estimate=pl.CostEstimate(
            flops=2 * m * rows * width * n,
            bytes_accessed=2 * rows * width * n,
            transcendentals=0,
        ),
        compiler_params=pltpu.CompilerParams(
            dimension_semantics=("arbitrary",), vmem_limit_bytes=VMEM_BYTES
        ),
    )(chunks, *arrays, down_weight)


def on_device(pool, ids, gate_q, up_q, gate_scale, up_scale, down_weight):
    n_fsdp = lax.axis_size("fsdp")
    n_tp = lax.axis_size("tp")
    f = lax.axis_index("fsdp")
    t = lax.axis_index("tp")
    rows_here = gate_q.shape[0]
    width = pool.shape[1]
    steps, step_rows = ids.shape
    members = n_fsdp // 2
    spans = n_fsdp // n_tp // 2
    q = f // 2
    core = f % 2
    near = levels()
    masks = [0] + [r for level in near for r in level]

    g = math.gcd(rows_here, BLOCK)
    row_blocks = (
        (f * n_tp + t) * rows_here + g * jnp.arange(rows_here // g, dtype=jnp.int32)
    ) // BLOCK
    weights = (gate_q, up_q) + tuple(
        jnp.repeat(jnp.take(s, row_blocks, axis=0), BLOCK, axis=1)
        for s in (gate_scale, up_scale)
    )

    share = steps * step_rows // n_tp
    by_owner = ids.reshape(steps, n_tp, step_rows // n_tp).transpose(1, 0, 2)
    by_owner = by_owner.reshape(n_tp, share)
    requests = jnp.arange(pool.shape[0], dtype=jnp.int32)

    def pick(begin, end, n_pieces):
        rr = (end - begin) // members
        named = by_owner[:, begin:end].reshape(n_tp, members, rr).transpose(1, 0, 2)
        chosen = (named.reshape(-1, 1) == requests).astype(jnp.bfloat16)
        size = width // n_pieces
        return [
            jnp.dot(
                chosen,
                pool[:, i * size : (i + 1) * size],
                preferred_element_type=jnp.float32,
            ).astype(jnp.bfloat16)
            for i in range(n_pieces)
        ]

    far = [r for level in near[1:] for r in level]
    visits = [(c, h) for c in range(2) for h in range(HALVES)]
    visits += [(r ^ c, h) for h in range(HALVES) for c in range(2) for r in near[0]]
    visits += [(r ^ c, h) for c in range(2) for r in far for h in range(HALVES)]
    flipped = f ^ jnp.array([r for r, _ in visits], dtype=jnp.int32)
    columns = flipped * HALVES + jnp.array([h for _, h in visits], dtype=jnp.int32)

    def wanted(got, core_flip, group, halves=range(HALVES)):
        found = []
        for r in group:
            for h in halves:
                pieces = got[r]
                if len(pieces) > 1:
                    found.append((r ^ core_flip, h, pieces[h], 0))
                else:
                    found.append((r ^ core_flip, h, pieces[0], h))
        return found

    def hold_all(found, *others):
        held = after([a for _, _, a, _ in found], *others)
        return [(r, h, a, j) for (r, h, _, j), a in zip(found, held)]

    def gate_up_part(found, acc, last):
        found = sorted(found, key=lambda w: visits.index(w[:2]))
        arrays, parts = [], []
        for _, _, a, j in found:
            if not any(a is b for b in arrays):
                arrays.append(a)
            parts.append(([a is b for b in arrays].index(True), j))
        at = visits.index(found[0][:2])
        return gate_up(
            width // HALVES, arrays, tuple(parts), at, columns, weights, acc, last
        )

    def scatter(hidden):
        pm = hidden.shape[0] // members
        pieces = [
            lax.dynamic_slice_in_dim(hidden, (q ^ (r // 2)) * pm, pm, axis=0)
            for r in range(0, n_fsdp, 2)
        ]
        return [swap(p, 2 * i) if i else p for i, p in enumerate(pieces)]

    def to_planes(pieces):
        pieces = jnp.stack(pieces)
        arrived = []
        for dz in range(n_tp):
            to = (t + dz) % n_tp
            for v in range(spans):
                piece = lax.dynamic_index_in_dim(
                    pieces, q ^ (to * spans + v), 0, keepdims=False
                )
                arrived.append(shift(piece, dz) if dz else piece)
        return arrived

    def down_part(by_core):
        n_here = n_tp * spans
        pm = by_core[0][0][0].shape[0] // n_here
        arrays, where, sources, chunks = [], {}, [], []
        for c, got in enumerate(by_core):
            for r in masks:
                where[c, r] = (len(arrays), len(got[r]))
                arrays.extend(got[r])
        for c in range(2):
            for i in range(n_here):
                parts = []
                for r in masks:
                    a, held = where[c, r]
                    each = n_here // held
                    parts.append((a + i // each, (i % each) * pm))
                sources.append(tuple(parts))
                dz, v = divmod(i, spans)
                chunks.append((2 * v + (core ^ c)) * n_tp + (t - dz) % n_tp)
        chunks = jnp.stack(chunks).astype(jnp.int32)
        return down(n_tp, rows_here, arrays, tuple(sources), pm, chunks, down_weight)

    def exchange(partial):
        rows = partial.shape[0] // n_tp
        shares = [
            lax.dynamic_slice_in_dim(partial, (t + dz) % n_tp * rows, rows, axis=0)
            for dz in range(n_tp)
        ]
        return [shift(s, dz) if dz else s for dz, s in enumerate(shares)]

    def total(shares):
        summed = functools.reduce(jnp.add, [s.astype(jnp.float32) for s in shares])
        rr = summed.shape[0] // members
        summed = summed.astype(jnp.bfloat16).reshape(members, rr, width)
        place = {r: i for i, r in enumerate(masks)}
        back = jnp.array([place[2 * i] for i in range(members)], dtype=jnp.int32)
        ordered = [
            lax.dynamic_index_in_dim(summed, back[q ^ i], 0, keepdims=False)
            for i in range(members)
        ]
        return jnp.concatenate(ordered)

    n = len(CHUNKS)
    ends = [share * sum(CHUNKS[: i + 1]) // sum(CHUNKS) for i in range(n)]
    first = {0: pick(0, ends[0], HALVES)}
    last = {0: pick(ends[0], ends[1], 1)}

    def blocks_of(got, group):
        return [got[r] for r in group]

    def hold(got, group, *others):
        for r, held in zip(group, after(blocks_of(got, group), *others)):
            got[r] = held

    def far_blocks(got, axis):
        for level in near[1:]:
            spread(got, level, axis)

    def land(pieces):
        got = {0: [jnp.concatenate(pieces)]}
        spread(got, near[0], 0)
        return got

    def twins_of(got, group):
        return {r: other_core(got[r]) for r in group}

    sent = []
    for h in range(HALVES):
        sent.append([swap(first[0][h], r) for r in near[0]])
    acc_first = gate_up_part(
        wanted(first, 0, [0]) + wanted(twins_of(first, [0]), 1, [0]), None, False
    )
    sent[0] = after(sent[0], acc_first)
    twins = {r: [swap(p, 1)] for r, p in zip(near[0], sent[0])}
    acc_last = wanted(last, 0, [0]) + wanted(twins_of(last, [0]), 1, [0])
    acc_last = gate_up_part(hold_all(acc_last, acc_first, sent[0]), None, False)
    pieces = [(r, 0, p, 0) for r, p in zip(near[0], sent[0])]
    pieces += [(r ^ 1, 0, twins[r][0], 0) for r in near[0]]
    acc_first = gate_up_part(hold_all(pieces, acc_last), acc_first, False)
    for h in range(1, HALVES):
        sent[h] = after(sent[h], acc_first)
    for i, r in enumerate(near[0]):
        first[r] = [sent[h][i] for h in range(HALVES)]
    far_blocks(first, 1)
    last[0] = after(last[0], sent[1:])
    spread(last, near[0], 1)
    for h in range(1, HALVES):
        pieces = [(r, h, p, 0) for r, p in zip(near[0], sent[h])]
        pieces += [(r ^ 1, h, swap(p, 1), 0) for r, p in zip(near[0], sent[h])]
        acc_first = gate_up_part(pieces, acc_first, False)
    hold(first, far, acc_first)
    pieces = wanted(first, 0, far) + wanted(twins_of(first, far), 1, far)
    hidden_first = gate_up_part(pieces, acc_first, True)
    moved_first = scatter(hidden_first)

    hold(last, near[0], moved_first)
    moved_first = to_planes(moved_first)
    far_blocks(last, 1)
    twins = twins_of(last, near[0])
    pieces = wanted(last, 0, near[0]) + wanted(twins, 1, near[0])
    acc_last = gate_up_part(hold_all(pieces, moved_first[0]), acc_last, False)
    hold(last, far, acc_last)
    landed_first = land(after(moved_first, acc_last))
    twins = twins_of(last, far)
    pieces = wanted(last, 0, far) + wanted(twins, 1, far)
    hidden_last = gate_up_part(pieces, acc_last, True)
    moved_last = scatter(hidden_last)

    hold(landed_first, near[0], moved_last[0])
    far_blocks(landed_first, 0)
    twins = twins_of(landed_first, [0] + near[0])
    moved_last = to_planes(moved_last)
    twins.update(twins_of(landed_first, far))
    partial_first = down_part(after((landed_first, twins), moved_last[0]))
    shares_first = exchange(partial_first)
    landed_last = land(after(moved_last, shares_first[0]))

    hold(landed_last, near[0], shares_first[0])
    far_blocks(landed_last, 0)
    twins = twins_of(landed_last, masks)
    shares_last = exchange(down_part((landed_last, twins)))
    shares_first, shares_last = after((shares_first, shares_last))
    mixed = jnp.concatenate([total(shares_first), total(shares_last)])
    return mixed.reshape(steps, share // steps, width)


def solution(mesh):
    in_specs = (
        P(None, "fsdp"),
        P(),
        P(("fsdp", "tp"), None),
        P(("fsdp", "tp"), None),
        P(),
        P(),
        P("tp", "fsdp"),
    )
    out_specs = P(None, "tp", "fsdp")

    return jax.shard_map(
        on_device, mesh=mesh, in_specs=in_specs, out_specs=out_specs, check_vma=False
    )
```
